256 devices in a mesh: row: 8 (over x, core), col: 32 (over z, y).
Axes of the slice: x: 4, y: 4, z: 8, core: 2. Of those that a mesh axis runs over, the one named last changes fastest.
Arguments:
- matrix: float32 [24576, 12288], P('row', 'col'), may hold values from -6 to 6
Outputs:
- updated: float32 [24576, 12288], P('row', 'col')
The draws below stay inside these ranges and needn't reach their ends.
All inputs are finite; a program needn't handle non-finite values.
Results may differ from the reference program's by a relative error of at most 0.0003.
Values sent between devices are 32-bit elements; how exact they have to be, the bound alone decides.
A program may use at most 64 MiB of HBM per device.

```python
import jax
import jax.numpy as jnp
from jax import lax

PANEL = 256
ROWS = 24576
COLS = 12288


def draw_matrix(key, part):
    base = jnp.clip(jax.random.normal(key, (ROWS, COLS), jnp.float32), -5.0, 5.0)
    shared = jnp.clip(jax.random.normal(jax.random.fold_in(key, 11), (ROWS, 1), jnp.float32), -5.0, 5.0)
    column = jnp.arange(COLS)[None, :]
    row_index = jnp.arange(ROWS)[:, None]
    in_panel = column < PANEL
    root_rows = jnp.sqrt(jnp.float32(ROWS))
    diagonal = jnp.where(in_panel & (row_index == column), 2.0, 0.0)
    position = column.astype(jnp.float32) / jnp.float32(PANEL - 1)
    decay = jnp.power(jnp.float32(0.3), jnp.minimum(position, 1.0))
    panel_part = decay * (base / root_rows + diagonal) + shared * (0.3 / root_rows)
    return jnp.where(in_panel, panel_part, base).astype(jnp.float32)


def setup_inputs(seed: int = 0) -> dict:
    key_list = jax.random.split(jax.random.key(seed), 2)
    matrix = draw_matrix(jax.random.fold_in(key_list[1], 71), 0)
    return {"matrix": matrix}


def reference(matrix):
    highest = lax.Precision.HIGHEST
    panel = matrix[:, :PANEL]
    basis, upper = jnp.linalg.qr(panel)
    signs = jnp.sign(jnp.diagonal(upper))
    basis = basis * signs[None, :]
    vectors = basis.at[:PANEL].add(jnp.eye(PANEL, dtype=basis.dtype))
    lead = vectors[:PANEL]
    projected = jnp.dot(vectors.T.astype(jnp.float32), matrix.astype(jnp.float32), precision=highest, preferred_element_type=jnp.float32)
    coeffs = jnp.linalg.solve(lead, projected)
    return matrix - jnp.dot(vectors.astype(jnp.float32), coeffs.astype(jnp.float32), precision=highest, preferred_element_type=jnp.float32)
```

```python
import functools

import jax
import jax.numpy as jnp
from jax import lax
from jax.experimental import pallas as pl
from jax.experimental.pallas import tpu as pltpu
from jax.sharding import PartitionSpec as P

PANEL = 256
Y, Z = 4, 8
ROW = 8
PIECE = 32
BLOCK = 64
MESH = pl.DeviceIdType.MESH
HIGHEST = lax.Precision.HIGHEST

TREES = (
    (205809287, 1078206464, 153162274, 1145052164),
    (2425421888, 2348828425, 538199108, 2291729160),
    (1646792752, 573083664, 1082827025, 536928418),
    (16943360, 294848740, 2252343432, 321257537),
)
DEPTHS = (
    (1515870810, 3552543676, 3221224912),
    (1515870810, 3647453556, 671088562),
    (1515870810, 2381649390, 4294962692),
    (1515870810, 3474847550, 1693450230),
)
LAG = 4


def signed(mask):
    return mask - (1 << 32) if mask >= 1 << 31 else mask


def passes(tree, direction, col):
    return (jnp.int32(signed(TREES[tree][direction])) >> col) & 1 == 1


def neighbour(col, direction):
    y, z = lax.rem(col, Y), lax.div(col, Y)
    if direction == 0:
        y = lax.rem(y + 1, Y)
    elif direction == 1:
        y = lax.rem(y + Y - 1, Y)
    elif direction == 2:
        z = lax.rem(z + 1, Z)
    else:
        z = lax.rem(z + Z - 1, Z)
    return z * Y + y


def dot_t(a, b):
    return lax.dot_general(
        a, b, (((0,), (0,)), ((), ())), precision=HIGHEST, preferred_element_type=jnp.float32
    )


def dot(a, b):
    return jnp.dot(a, b, precision=HIGHEST, preferred_element_type=jnp.float32)


def tree_send(buf, send_sems, recv_sems, tree, direction, index, rows, col):
    row = lax.axis_index("row")
    return pltpu.make_async_remote_copy(
        src_ref=buf.at[rows],
        dst_ref=buf.at[rows],
        send_sem=send_sems.at[tree, direction],
        recv_sem=recv_sems.at[tree, index],
        device_id=(row, neighbour(col, direction)),
        device_id_type=MESH,
    )


def bit(mask, col):
    return (jnp.int32(signed(mask)) >> col) & 1


def depth_of(tree, col):
    return sum(bit(mask, col) << b for b, mask in enumerate(DEPTHS[tree]))


def tree_forward(buf, send_sems, recv_sems, step, count, piece, depths, col):
    for tree in range(4):
        index = step - LAG * depths[tree]
        rows = pl.ds(pl.multiple_of((index * 4 + tree) * piece, piece), piece)

        @pl.when((index >= 0) & (index < count))
        def _():
            @pl.when(col != 0)
            def _():
                pltpu.make_async_copy(buf.at[rows], buf.at[rows], recv_sems.at[tree, index]).wait()

            for direction in range(4):

                @pl.when(passes(tree, direction, col))
                def _():
                    tree_send(buf, send_sems, recv_sems, tree, direction, index, rows, col).start()


def tree_drain(buf, send_sems, recv_sems, total, col):
    for tree in range(4):
        for direction in range(4):

            @pl.when(passes(tree, direction, col))
            def _():
                tree_send(
                    buf, send_sems, recv_sems, tree, direction, 0, pl.ds(0, total), col
                ).wait_send()


def gather_kernel(
    a_hbm,
    p_hbm,
    g_out,
    top_out,
    a,
    p,
    part,
    slots,
    total,
    top,
    tree_sends,
    tree_recvs,
    rs_sends,
    rs_recvs,
    ag_sends,
    ag_recvs,
    top_sends,
    top_recv,
    local_sems,
):
    row, col = lax.axis_index("row"), lax.axis_index("col")
    rows, width = a.shape
    share = PANEL // ROW
    macro = PANEL
    count = rows // macro
    per_macro = macro // (4 * PIECE)

    panel_copy = pltpu.make_async_copy(a_hbm.at[:, pl.ds(0, PANEL)], p, local_sems.at[0])
    loads = [
        pltpu.make_async_copy(
            a_hbm.at[pl.ds(i * PANEL, PANEL)], a.at[pl.ds(i * PANEL, PANEL)], local_sems.at[1 + i]
        )
        for i in range(count)
    ]

    @pl.when(col == 0)
    def _():
        panel_copy.start()

    for load in loads:
        load.start()

    barrier = pltpu.get_barrier_semaphore()
    peers = [lax.rem(row + d, ROW) for d in range(1, ROW)]
    for peer in peers:
        pl.semaphore_signal(barrier, inc=1, device_id=(peer, col), device_id_type=MESH)
    for direction in range(4):
        pl.semaphore_signal(
            barrier, inc=1, device_id=(row, neighbour(col, direction)), device_id_type=MESH
        )
    pl.semaphore_wait(barrier, len(peers) + 4)

    def top_copy(d):
        return pltpu.make_async_remote_copy(
            src_ref=a.at[pl.ds(0, PANEL)],
            dst_ref=top,
            send_sem=top_sends.at[d],
            recv_sem=top_recv,
            device_id=(peers[d], col),
            device_id_type=MESH,
        )

    loads[0].wait()

    @pl.when((row == 0) & (col != 0))
    def _():
        for d in range(ROW - 1):
            top_copy(d).start()

    @pl.when(col == 0)
    def _():
        panel_copy.wait()

    for load in loads[1:]:
        load.wait()

    part[...] = jnp.zeros_like(part)

    depths = [depth_of(tree, col) for tree in range(4)]
    deepest = functools.reduce(jnp.maximum, depths)
    pieces = count * per_macro

    @pl.loop(0, pieces + LAG * deepest)
    def _(step):
        tree_forward(p, tree_sends, tree_recvs, step, pieces, PIECE, depths, col)
        due = step - LAG * deepest + 1

        @pl.when((due > 0) & (lax.rem(due, per_macro) == 0))
        def _():
            i = lax.div(due, per_macro) - 1
            block = pl.ds(pl.multiple_of(i * macro, macro), macro)
            part[...] += dot_t(p[block], a[block])
            pltpu.make_async_copy(p.at[block], p_hbm.at[block], local_sems.at[0]).start()

    def part_copy(d):
        return pltpu.make_async_remote_copy(
            src_ref=part.at[pl.ds(pl.multiple_of(peers[d] * share, share), share)],
            dst_ref=slots.at[d],
            send_sem=rs_sends.at[d],
            recv_sem=rs_recvs.at[d],
            device_id=(peers[d], col),
            device_id_type=MESH,
        )

    mine = pl.ds(pl.multiple_of(row * share, share), share)

    def sum_copy(d):
        return pltpu.make_async_remote_copy(
            src_ref=total.at[mine],
            dst_ref=total.at[mine],
            send_sem=ag_sends.at[d],
            recv_sem=ag_recvs.at[d],
            device_id=(peers[d], col),
            device_id_type=MESH,
        )

    for d in range(ROW - 1):
        part_copy(d).start()

    @pl.when((row == 0) & (col == 0))
    def _():
        for d in range(ROW - 1):
            top_copy(d).start()

    acc = part[mine]
    for d in range(ROW - 1):
        part_copy(d).wait_recv()
        acc += slots[d]
    total[mine] = acc
    for d in range(ROW - 1):
        sum_copy(d).start()
    for d in range(ROW - 1):
        sum_copy(d).wait_recv()
    g_out[...] = total[...]

    @pl.when(row != 0)
    def _():
        top_copy(0).wait_recv()
        top_out[...] = top[...]

    @pl.when(row == 0)
    def _():
        top_out[...] = a[pl.ds(0, PANEL)]
        for d in range(ROW - 1):
            top_copy(d).wait_send()

    for d in range(ROW - 1):
        part_copy(d).wait_send()
        sum_copy(d).wait_send()
    tree_drain(p, tree_sends, tree_recvs, rows // 4, col)
    pltpu.make_async_copy(p, p_hbm, local_sems.at[0]).wait()


def gather(matrix):
    rows, width = matrix.shape
    count = rows // PANEL
    dma = pltpu.SemaphoreType.DMA
    return pl.pallas_call(
        gather_kernel,
        name="gather",
        out_shape=(
            jax.ShapeDtypeStruct((rows, PANEL), jnp.float32),
            jax.ShapeDtypeStruct((PANEL, width), jnp.float32),
            jax.ShapeDtypeStruct((PANEL, width), jnp.float32),
        ),
        in_specs=[pl.BlockSpec(memory_space=pl.ANY)],
        out_specs=(
            pl.BlockSpec(memory_space=pl.ANY),
            pl.BlockSpec(memory_space=pltpu.VMEM),
            pl.BlockSpec(memory_space=pltpu.VMEM),
        ),
        scratch_shapes=[
            pltpu.VMEM((rows, width), jnp.float32),
            pltpu.VMEM((rows, PANEL), jnp.float32),
            pltpu.VMEM((PANEL, width), jnp.float32),
            pltpu.VMEM((ROW - 1, PANEL // ROW, width), jnp.float32),
            pltpu.VMEM((PANEL, width), jnp.float32),
            pltpu.VMEM((PANEL, width), jnp.float32),
            dma((4, 4)),
            dma((4, rows // (4 * PIECE))),
            dma((ROW - 1,)),
            dma((ROW - 1,)),
            dma((ROW - 1,)),
            dma((ROW - 1,)),
            dma((ROW - 1,)),
            dma(()),
            dma((1 + count,)),
        ],
        compiler_params=pltpu.CompilerParams(
            collective_id=0, has_side_effects=True, vmem_limit_bytes=48 << 20
        ),
    )(matrix)


def eliminate(block, full):
    size, width = block.shape
    index = lax.broadcasted_iota(jnp.int32, (size, 1), 0)
    pivots = jnp.zeros((size, 1), jnp.float32)
    for k in range(size):
        column = block[:, k : k + 1]
        row = block[k : k + 1, :]
        pivot = block[k : k + 1, k : k + 1]
        keep = index != k if full else index > k
        factor = jnp.where(keep, column, 0.0) * (1.0 / pivot)
        pivots = jnp.where(index == k, pivot, pivots)
        block = block - factor * row
    return block, pivots


def factor_kernel(g, top, out, chol, gj):
    @pl.when(lax.axis_index("col") == 0)
    def _():
        b = BLOCK
        blocks = PANEL // b
        eye = jnp.eye(b, dtype=jnp.float32)
        chol[...] = jnp.zeros_like(chol)
        gj[...] = jnp.zeros_like(gj)

        def chol_block(j):
            lo, hi = j * b, (j + 1) * b
            sym = g[lo:hi, :PANEL]
            if j == 0:
                left, right = sym, None
            else:
                prod = dot_t(chol[:lo, lo:hi], chol[:lo, :])
                left, right = sym - prod[:, :PANEL], -prod[:, PANEL : PANEL + lo]
            done, pivots = eliminate(jnp.concatenate([left[:, lo:hi], eye], axis=1), False)
            inv = done[:, b:] * lax.rsqrt(pivots)
            parts = [left[:, lo:]]
            if right is not None:
                parts.append(right)
            parts.append(eye)
            res = dot(inv, jnp.concatenate(parts, axis=1))
            chol[lo:hi, lo : PANEL + hi] = res

        def gj_block(j):
            lo, hi = j * b, (j + 1) * b
            rowk = chol[lo:hi, :PANEL] + top[lo:hi, :PANEL]
            if j == 0:
                work = rowk
                right = None
            else:
                prod = dot(rowk[:, :lo], gj[:lo, :])
                work = rowk - prod[:, :PANEL]
                right = -prod[:, PANEL : PANEL + lo]
            done, pivots = eliminate(jnp.concatenate([work[:, lo:hi], eye], axis=1), True)
            inv = done[:, b:] * (1.0 / pivots)
            parts = [work[:, lo:]]
            if right is not None:
                parts.append(right)
            parts.append(eye)
            new = dot(inv, jnp.concatenate(parts, axis=1))
            if j > 0:
                gj[:lo, lo : PANEL + hi] -= dot(gj[:lo, lo:hi], new)
            gj[lo:hi, lo : PANEL + hi] = new

        for step in range(blocks + 1):
            if step < blocks:
                chol_block(step)
            if step > 0:
                gj_block(step - 1)
        out[:PANEL] = chol[:, PANEL:]
        out[PANEL:] = gj[:, PANEL:]


def factor(g, top):
    vmem = pl.BlockSpec(memory_space=pltpu.VMEM)
    return pl.pallas_call(
        factor_kernel,
        name="factor",
        out_shape=jax.ShapeDtypeStruct((2 * PANEL, PANEL), jnp.float32),
        in_specs=[vmem, vmem],
        out_specs=vmem,
        scratch_shapes=[
            pltpu.VMEM((PANEL, 2 * PANEL), jnp.float32),
            pltpu.VMEM((PANEL, 2 * PANEL), jnp.float32),
        ],
    )(g, top)


SMALL = 16


def spread_kernel(f_hbm, g, top, z_out, x_out, f, tree_sends, tree_recvs, local_sem):
    row, col = lax.axis_index("row"), lax.axis_index("col")
    load = pltpu.make_async_copy(f_hbm, f, local_sem)

    @pl.when(col == 0)
    def _():
        load.start()

    barrier = pltpu.get_barrier_semaphore()
    for direction in range(4):
        pl.semaphore_signal(
            barrier, inc=1, device_id=(row, neighbour(col, direction)), device_id_type=MESH
        )
    pl.semaphore_wait(barrier, 4)

    @pl.when(col == 0)
    def _():
        load.wait()

    count = 2 * PANEL // (4 * SMALL)
    depths = [depth_of(tree, col) for tree in range(4)]
    deepest = functools.reduce(jnp.maximum, depths)

    @pl.loop(0, count + LAG * deepest)
    def _(step):
        tree_forward(f, tree_sends, tree_recvs, step, count, SMALL, depths, col)

    z = dot(f[:PANEL], g[...])
    z_out[...] = z
    x_out[...] = dot(f[PANEL:], z + top[...])
    tree_drain(f, tree_sends, tree_recvs, 2 * PANEL // 4, col)


def spread(factors, g, top):
    vmem = pl.BlockSpec(memory_space=pltpu.VMEM)
    dma = pltpu.SemaphoreType.DMA
    shape = jax.ShapeDtypeStruct(g.shape, jnp.float32)
    return pl.pallas_call(
        spread_kernel,
        name="spread",
        out_shape=(shape, shape),
        in_specs=[pl.BlockSpec(memory_space=pl.ANY), vmem, vmem],
        out_specs=(vmem, vmem),
        scratch_shapes=[
            pltpu.VMEM((2 * PANEL, PANEL), jnp.float32),
            dma((4, 4)),
            dma((4, 2 * PANEL // (4 * SMALL))),
            dma(()),
        ],
        compiler_params=pltpu.CompilerParams(collective_id=1, has_side_effects=True),
    )(factors, g, top)


TILE = 512


def update_kernel(a, p, z, x, out):
    out[...] = a[...] - dot(p[...], x[...])

    @pl.when((lax.axis_index("row") == 0) & (pl.program_id(0) == 0))
    def _():
        out[:PANEL] = -z[...]


def update(matrix, panel, z, x):
    rows, width = matrix.shape
    whole = pl.BlockSpec((PANEL, width), lambda i: (0, 0))
    return pl.pallas_call(
        update_kernel,
        name="update",
        out_shape=jax.ShapeDtypeStruct(matrix.shape, jnp.float32),
        grid=(rows // TILE,),
        in_specs=[
            pl.BlockSpec((TILE, width), lambda i: (i, 0)),
            pl.BlockSpec((TILE, PANEL), lambda i: (i, 0)),
            whole,
            whole,
        ],
        out_specs=pl.BlockSpec((TILE, width), lambda i: (i, 0)),
    )(matrix, panel, z, x)


def on_device(matrix):
    panel, g, top = gather(matrix)
    factors = factor(g, top)
    z, x = spread(factors, g, top)
    return update(matrix, panel, z, x)


def solution(mesh):
    in_specs = (P("row", "col"),)
    out_specs = P("row", "col")
    return jax.shard_map(
        on_device, mesh=mesh, in_specs=in_specs, out_specs=out_specs, check_vma=False
    )
```

```python
import functools

import jax
import jax.numpy as jnp
from jax import lax
from jax.experimental import pallas as pl
from jax.experimental.pallas import tpu as pltpu
from jax.sharding import PartitionSpec as P

PANEL = 256
Y, Z = 4, 8
ROW = 8
PIECE = 32
BLOCK = 32
MESH = pl.DeviceIdType.MESH
HIGHEST = lax.Precision.HIGHEST

TREES = (
    (205809287, 1078206464, 153162274, 1145052164),
    (2425421888, 2348828425, 538199108, 2291729160),
    (1646792752, 573083664, 1082827025, 536928418),
    (16943360, 294848740, 2252343432, 321257537),
)
DEPTHS = (
    (1515870810, 3552543676, 3221224912),
    (1515870810, 3647453556, 671088562),
    (1515870810, 2381649390, 4294962692),
    (1515870810, 3474847550, 1693450230),
)
TOP_STEP = 8
LAG = 4


def signed(mask):
    return mask - (1 << 32) if mask >= 1 << 31 else mask


def passes(tree, direction, col):
    return (jnp.int32(signed(TREES[tree][direction])) >> col) & 1 == 1


def neighbour(col, direction):
    y, z = lax.rem(col, Y), lax.div(col, Y)
    if direction == 0:
        y = lax.rem(y + 1, Y)
    elif direction == 1:
        y = lax.rem(y + Y - 1, Y)
    elif direction == 2:
        z = lax.rem(z + 1, Z)
    else:
        z = lax.rem(z + Z - 1, Z)
    return z * Y + y


def dot_t(a, b):
    return lax.dot_general(
        a, b, (((0,), (0,)), ((), ())), precision=HIGHEST, preferred_element_type=jnp.float32
    )


def split2(x):
    high = x.astype(jnp.bfloat16)
    return high, (x - high.astype(jnp.float32)).astype(jnp.bfloat16)


def dot_split(a, b):
    a_high, a_low = split2(a)
    b_high, b_low = split2(b)
    return jnp.dot(
        jnp.concatenate([a_high, a_low, a_high], axis=1),
        jnp.concatenate([b_high, b_high, b_low], axis=0),
        preferred_element_type=jnp.float32,
    )


def dot(a, b):
    return jnp.dot(a, b, precision=HIGHEST, preferred_element_type=jnp.float32)


def tree_send(buf, send_sems, recv_sems, tree, direction, index, rows, col):
    row = lax.axis_index("row")
    return pltpu.make_async_remote_copy(
        src_ref=buf.at[rows],
        dst_ref=buf.at[rows],
        send_sem=send_sems.at[tree, direction],
        recv_sem=recv_sems.at[tree, index],
        device_id=(row, neighbour(col, direction)),
        device_id_type=MESH,
    )


def bit(mask, col):
    return (jnp.int32(signed(mask)) >> col) & 1


def depth_of(tree, col):
    return sum(bit(mask, col) << b for b, mask in enumerate(DEPTHS[tree]))


def tree_forward(buf, send_sems, recv_sems, step, count, piece, lag, depths, col):
    for tree in range(4):
        index = step - lag * depths[tree]
        rows = pl.ds(pl.multiple_of((index * 4 + tree) * piece, piece), piece)

        @pl.when((index >= 0) & (index < count))
        def _():
            @pl.when(col != 0)
            def _():
                pltpu.make_async_copy(buf.at[rows], buf.at[rows], recv_sems.at[tree, index]).wait()

            for direction in range(4):

                @pl.when(passes(tree, direction, col))
                def _():
                    tree_send(buf, send_sems, recv_sems, tree, direction, index, rows, col).start()


def tree_drain(buf, send_sems, recv_sems, total, col):
    for tree in range(4):
        for direction in range(4):

            @pl.when(passes(tree, direction, col))
            def _():
                tree_send(
                    buf, send_sems, recv_sems, tree, direction, 0, pl.ds(0, total), col
                ).wait_send()


def gather_kernel(
    a_hbm,
    p_hbm,
    g_out,
    top_out,
    a,
    p,
    part,
    slots,
    total,
    top,
    tree_sends,
    tree_recvs,
    rs_sends,
    rs_recvs,
    ag_sends,
    ag_recvs,
    share_sends,
    share_recv,
    top_sends,
    top_recvs,
    local_sems,
):
    row, col = lax.axis_index("row"), lax.axis_index("col")
    rows, width = a.shape
    share = PANEL // ROW
    macro = PANEL
    count = rows // macro
    per_macro = macro // (4 * PIECE)

    panel_copy = pltpu.make_async_copy(a_hbm.at[:, pl.ds(0, PANEL)], p, local_sems.at[0])
    loads = [
        pltpu.make_async_copy(
            a_hbm.at[pl.ds(i * PANEL, PANEL)], a.at[pl.ds(i * PANEL, PANEL)], local_sems.at[1 + i]
        )
        for i in range(count)
    ]

    @pl.when(col == 0)
    def _():
        panel_copy.start()

    for load in loads:
        load.start()

    barrier = pltpu.get_barrier_semaphore()
    peers = [lax.rem(row + d, ROW) for d in range(1, ROW)]
    for peer in peers:
        pl.semaphore_signal(barrier, inc=1, device_id=(peer, col), device_id_type=MESH)
    for direction in range(4):
        pl.semaphore_signal(
            barrier, inc=1, device_id=(row, neighbour(col, direction)), device_id_type=MESH
        )
    pl.semaphore_wait(barrier, len(peers) + 4)

    mine = pl.ds(pl.multiple_of(row * share, share), share)

    def share_copy(d):
        theirs = pl.ds(pl.multiple_of(peers[d] * share, share), share)
        return pltpu.make_async_remote_copy(
            src_ref=a.at[theirs],
            dst_ref=top.at[theirs],
            send_sem=share_sends.at[d],
            recv_sem=share_recv,
            device_id=(peers[d], col),
            device_id_type=MESH,
        )

    own_share = pltpu.make_async_copy(a.at[mine], top.at[mine], share_recv)

    def top_copy(d):
        return pltpu.make_async_remote_copy(
            src_ref=top.at[mine],
            dst_ref=top.at[mine],
            send_sem=top_sends.at[d],
            recv_sem=top_recvs.at[d],
            device_id=(peers[d], col),
            device_id_type=MESH,
        )

    loads[0].wait()

    @pl.when(row == 0)
    def _():
        own_share.start()
        for d in range(ROW - 1):
            share_copy(d).start()

    @pl.when(col == 0)
    def _():
        panel_copy.wait()

    for load in loads[1:]:
        load.wait()

    part[...] = jnp.zeros_like(part)

    depths = [depth_of(tree, col) for tree in range(4)]
    deepest = functools.reduce(jnp.maximum, depths)
    pieces = count * per_macro

    @pl.loop(0, pieces + LAG * deepest)
    def _(step):
        tree_forward(p, tree_sends, tree_recvs, step, pieces, PIECE, LAG, depths, col)
        due = step - LAG * deepest + 1

        @pl.when(step == TOP_STEP)
        def _():
            own_share.wait()
            for d in range(ROW - 1):
                top_copy(d).start()

        @pl.when((due > 0) & (lax.rem(due, per_macro) == 0))
        def _():
            i = lax.div(due, per_macro) - 1
            block = pl.ds(pl.multiple_of(i * macro, macro), macro)
            part[...] += dot_t(p[block], a[block])
            pltpu.make_async_copy(p.at[block], p_hbm.at[block], local_sems.at[0]).start()

    def part_copy(d):
        return pltpu.make_async_remote_copy(
            src_ref=part.at[pl.ds(pl.multiple_of(peers[d] * share, share), share)],
            dst_ref=slots.at[d],
            send_sem=rs_sends.at[d],
            recv_sem=rs_recvs.at[d],
            device_id=(peers[d], col),
            device_id_type=MESH,
        )

    def sum_copy(d):
        return pltpu.make_async_remote_copy(
            src_ref=total.at[mine],
            dst_ref=total.at[mine],
            send_sem=ag_sends.at[d],
            recv_sem=ag_recvs.at[d],
            device_id=(peers[d], col),
            device_id_type=MESH,
        )

    for d in range(ROW - 1):
        part_copy(d).start()

    acc = part[mine]
    for d in range(ROW - 1):
        part_copy(d).wait_recv()
        acc += slots[d]
    total[mine] = acc
    for d in range(ROW - 1):
        sum_copy(d).start()
    for d in range(ROW - 1):
        sum_copy(d).wait_recv()
    g_out[...] = total[...]

    for d in range(ROW - 1):
        top_copy(d).wait_recv()
        top_copy(d).wait_send()
    top_out[...] = top[...]

    @pl.when(row == 0)
    def _():
        for d in range(ROW - 1):
            share_copy(d).wait_send()

    for d in range(ROW - 1):
        part_copy(d).wait_send()
        sum_copy(d).wait_send()
    tree_drain(p, tree_sends, tree_recvs, rows // 4, col)
    pltpu.make_async_copy(p, p_hbm, local_sems.at[0]).wait()


def gather(matrix):
    rows, width = matrix.shape
    count = rows // PANEL
    dma = pltpu.SemaphoreType.DMA
    return pl.pallas_call(
        gather_kernel,
        name="gather",
        out_shape=(
            jax.ShapeDtypeStruct((rows, PANEL), jnp.float32),
            jax.ShapeDtypeStruct((PANEL, width), jnp.float32),
            jax.ShapeDtypeStruct((PANEL, width), jnp.float32),
        ),
        in_specs=[pl.BlockSpec(memory_space=pl.ANY)],
        out_specs=(
            pl.BlockSpec(memory_space=pl.ANY),
            pl.BlockSpec(memory_space=pltpu.VMEM),
            pl.BlockSpec(memory_space=pltpu.VMEM),
        ),
        scratch_shapes=[
            pltpu.VMEM((rows, width), jnp.float32),
            pltpu.VMEM((rows, PANEL), jnp.float32),
            pltpu.VMEM((PANEL, width), jnp.float32),
            pltpu.VMEM((ROW - 1, PANEL // ROW, width), jnp.float32),
            pltpu.VMEM((PANEL, width), jnp.float32),
            pltpu.VMEM((PANEL, width), jnp.float32),
            dma((4, 4)),
            dma((4, rows // (4 * PIECE))),
            dma((ROW - 1,)),
            dma((ROW - 1,)),
            dma((ROW - 1,)),
            dma((ROW - 1,)),
            dma((ROW - 1,)),
            dma(()),
            dma((ROW - 1,)),
            dma((ROW - 1,)),
            dma((1 + count,)),
        ],
        compiler_params=pltpu.CompilerParams(
            collective_id=0, has_side_effects=True, vmem_limit_bytes=48 << 20
        ),
    )(matrix)


def invert_pair(one, two):
    half = one.shape[0]
    width = 128
    spare = [jnp.zeros((8, width - 2 * half), jnp.float32)] if width > 2 * half else []
    xs = [
        jnp.concatenate([one[i : i + 8], two[i : i + 8]] + spare, axis=1)
        for i in range(0, half, 8)
    ]
    lane = lax.broadcasted_iota(jnp.int32, (8, width), 1)
    index = lax.broadcasted_iota(jnp.int32, (8, width), 0)
    right = lane >= half
    offset = lax.rem(lane, half)
    base = lane - offset
    right_row, offset_row = right[:1], offset[:1]

    def column(x, k):
        return jnp.take_along_axis(x, base + k, axis=1)

    for k in range(0, half, 2):
        home, s = k // 8, k % 8
        c0 = [column(x, k) for x in xs]
        c1 = [column(x, k + 1) for x in xs]
        a, b = c0[home][s : s + 1], c1[home][s : s + 1]
        c, d = c0[home][s + 1 : s + 2], c1[home][s + 1 : s + 2]
        det = a * d - b * c
        inv = 1.0 / det
        in_pair = (offset == k) | (offset == k + 1)
        first, second = offset_row == k, offset_row == k + 1
        r0, r1 = xs[home][s : s + 1], xs[home][s + 1 : s + 2]
        r0 = jnp.where(first, 1.0, jnp.where(second, 0.0, r0))
        r1 = jnp.where(first, 0.0, jnp.where(second, 1.0, r1))
        w0 = (d * r0 - b * r1) * inv
        w1 = (a * r1 - c * r0) * inv
        w0b, w1b = jnp.broadcast_to(w0, (8, width)), jnp.broadcast_to(w1, (8, width))
        u0b, u1b = jnp.where(right, w0b, 0.0), jnp.where(right, w1b, 0.0)
        clear = in_pair & right
        ra = lax.rsqrt(a)
        top = jnp.broadcast_to(jnp.where(right_row, w0, r0 * ra), (8, width))
        low = jnp.broadcast_to(
            w1 * jnp.where(right_row, 1.0, ra * jnp.sqrt(jnp.where(right_row, 1.0, det))),
            (8, width),
        )
        for i, x in enumerate(xs):
            if i < home:
                new = jnp.where(clear, 0.0, x) - (c0[i] * u0b + c1[i] * u1b)
            elif i > home:
                new = jnp.where(in_pair, 0.0, x) - (c0[i] * w0b + c1[i] * w1b)
            else:
                moves = right | (index > s)
                new = jnp.where(in_pair & moves, 0.0, x) - jnp.where(
                    moves, c0[i] * w0b + c1[i] * w1b, 0.0
                )
                new = jnp.where(index == s, top, new)
                new = jnp.where(index == s + 1, low, new)
            xs[i] = new
    return jnp.concatenate(xs, axis=0)


def factor_kernel(g, top, out, chol, gj):
    @pl.when(lax.axis_index("col") == 0)
    def _():
        b = BLOCK
        blocks = PANEL // b
        eye = jnp.eye(b, dtype=jnp.float32)
        lower = lax.broadcasted_iota(jnp.int32, (b, b), 0) >= lax.broadcasted_iota(
            jnp.int32, (b, b), 1
        )
        chol[...] = jnp.zeros_like(chol)
        gj[...] = jnp.zeros_like(gj)

        for step in range(blocks + 1):
            one, two = eye, eye
            if step < blocks:
                lo, hi = step * b, (step + 1) * b
                left = g[lo:hi, lo:PANEL]
                wide = [left]
                if step > 0:
                    prod = dot_t(chol[:lo, lo:hi], chol[:lo, lo : PANEL + lo])
                    left = left - prod[:, : PANEL - lo]
                    wide = [left, -prod[:, PANEL - lo :]]
                wide.append(eye)
                one = left[:, :b]
            if step > 0:
                glo, ghi = (step - 1) * b, step * b
                work = chol[glo:ghi, :PANEL] + top[glo:ghi, :PANEL]
                gwide = [work]
                if glo > 0:
                    prod = dot(work[:, :glo], gj[:glo, glo : PANEL + glo])
                    work = work[:, glo:] - prod[:, : PANEL - glo]
                    gwide = [work, -prod[:, PANEL - glo :]]
                gwide.append(eye)
                two = work[:, :b]
            both = invert_pair(one, two)
            if step < blocks:
                inv = jnp.where(lower, both[:, :b], 0.0)
                chol[lo:hi, lo : PANEL + hi] = dot(inv, jnp.concatenate(wide, axis=1))
            if step > 0:
                new = dot(both[:, b : 2 * b], jnp.concatenate(gwide, axis=1))
                if glo > 0:
                    gj[:glo, glo : PANEL + ghi] -= dot(gj[:glo, glo:ghi], new)
                gj[glo:ghi, glo : PANEL + ghi] = new
        out[:PANEL] = chol[:, PANEL:]
        out[PANEL:] = gj[:, PANEL:]


def factor(g, top):
    vmem = pl.BlockSpec(memory_space=pltpu.VMEM)
    return pl.pallas_call(
        factor_kernel,
        name="factor",
        out_shape=jax.ShapeDtypeStruct((2 * PANEL, PANEL), jnp.float32),
        in_specs=[vmem, vmem],
        out_specs=vmem,
        scratch_shapes=[
            pltpu.VMEM((PANEL, 2 * PANEL), jnp.float32),
            pltpu.VMEM((PANEL, 2 * PANEL), jnp.float32),
        ],
    )(g, top)


SMALL = 16
SMALL_LAG = 7


def spread_kernel(f_hbm, g, top, z_out, x_out, f, tree_sends, tree_recvs, local_sem):
    row, col = lax.axis_index("row"), lax.axis_index("col")
    load = pltpu.make_async_copy(f_hbm, f, local_sem)

    @pl.when(col == 0)
    def _():
        load.start()

    barrier = pltpu.get_barrier_semaphore()
    for direction in range(4):
        pl.semaphore_signal(
            barrier, inc=1, device_id=(row, neighbour(col, direction)), device_id_type=MESH
        )
    pl.semaphore_wait(barrier, 4)

    @pl.when(col == 0)
    def _():
        load.wait()

    count = 2 * PANEL // (4 * SMALL)
    depths = [depth_of(tree, col) for tree in range(4)]
    deepest = functools.reduce(jnp.maximum, depths)

    @pl.loop(0, count + SMALL_LAG * deepest)
    def _(step):
        tree_forward(f, tree_sends, tree_recvs, step, count, SMALL, SMALL_LAG, depths, col)

    z = dot_split(f[:PANEL], g[...])
    z_out[...] = z
    x_out[...] = dot_split(f[PANEL:], z + top[...])
    tree_drain(f, tree_sends, tree_recvs, 2 * PANEL // 4, col)


def spread(factors, g, top):
    vmem = pl.BlockSpec(memory_space=pltpu.VMEM)
    dma = pltpu.SemaphoreType.DMA
    shape = jax.ShapeDtypeStruct(g.shape, jnp.float32)
    return pl.pallas_call(
        spread_kernel,
        name="spread",
        out_shape=(shape, shape),
        in_specs=[pl.BlockSpec(memory_space=pl.ANY), vmem, vmem],
        out_specs=(vmem, vmem),
        scratch_shapes=[
            pltpu.VMEM((2 * PANEL, PANEL), jnp.float32),
            dma((4, 4)),
            dma((4, 2 * PANEL // (4 * SMALL))),
            dma(()),
        ],
        compiler_params=pltpu.CompilerParams(collective_id=1, has_side_effects=True),
    )(factors, g, top)


TILE = 512


def update_kernel(a, p, z, x, out):
    out[...] = a[...] - dot_split(p[...], x[...])

    @pl.when((lax.axis_index("row") == 0) & (pl.program_id(0) == 0))
    def _():
        out[:PANEL] = -z[...]


def update(matrix, panel, z, x):
    rows, width = matrix.shape
    whole = pl.BlockSpec((PANEL, width), lambda i: (0, 0))
    return pl.pallas_call(
        update_kernel,
        name="update",
        out_shape=jax.ShapeDtypeStruct(matrix.shape, jnp.float32),
        grid=(rows // TILE,),
        in_specs=[
            pl.BlockSpec((TILE, width), lambda i: (i, 0)),
            pl.BlockSpec((TILE, PANEL), lambda i: (i, 0)),
            whole,
            whole,
        ],
        out_specs=pl.BlockSpec((TILE, width), lambda i: (i, 0)),
    )(matrix, panel, z, x)


def on_device(matrix):
    panel, g, top = gather(matrix)
    factors = factor(g, top)
    z, x = spread(factors, g, top)
    return update(matrix, panel, z, x)


def solution(mesh):
    in_specs = (P("row", "col"),)
    out_specs = P("row", "col")
    return jax.shard_map(
        on_device, mesh=mesh, in_specs=in_specs, out_specs=out_specs, check_vma=False
    )
```

```python
import functools

import jax
import jax.numpy as jnp
from jax import lax
from jax.experimental import pallas as pl
from jax.experimental.pallas import tpu as pltpu
from jax.sharding import PartitionSpec as P

PANEL = 256
Y, Z = 4, 8
ROW = 8
PIECE = 32
BLOCK = 32
SMALL = 32
SMALL_LAG = 4
MESH = pl.DeviceIdType.MESH
HIGHEST = lax.Precision.HIGHEST

TREES = (
    (205809287, 1078206464, 153162274, 1145052164),
    (2425421888, 2348828425, 538199108, 2291729160),
    (1646792752, 573083664, 1082827025, 536928418),
    (16943360, 294848740, 2252343432, 321257537),
)
DEPTHS = (
    (1515870810, 3552543676, 3221224912),
    (1515870810, 3647453556, 671088562),
    (1515870810, 2381649390, 4294962692),
    (1515870810, 3474847550, 1693450230),
)
TOP_STEP = 8
LAG = 4


def signed(mask):
    return mask - (1 << 32) if mask >= 1 << 31 else mask


def passes(tree, direction, col):
    return (jnp.int32(signed(TREES[tree][direction])) >> col) & 1 == 1


def neighbour(col, direction):
    y, z = lax.rem(col, Y), lax.div(col, Y)
    if direction == 0:
        y = lax.rem(y + 1, Y)
    elif direction == 1:
        y = lax.rem(y + Y - 1, Y)
    elif direction == 2:
        z = lax.rem(z + 1, Z)
    else:
        z = lax.rem(z + Z - 1, Z)
    return z * Y + y


def dot_t(a, b):
    precision = HIGHEST if a.dtype == jnp.float32 else None
    return lax.dot_general(
        a, b, (((0,), (0,)), ((), ())), precision=precision, preferred_element_type=jnp.float32
    )


def split2(x):
    high = x.astype(jnp.bfloat16)
    return high, (x - high.astype(jnp.float32)).astype(jnp.bfloat16)


def dot_split(a, b):
    a_high, a_low = split2(a)
    b_high, b_low = split2(b)
    return jnp.dot(
        jnp.concatenate([a_high, a_low, a_high], axis=1),
        jnp.concatenate([b_high, b_high, b_low], axis=0),
        preferred_element_type=jnp.float32,
    )


def dot_t_split(a, b):
    a_high, a_low = split2(a)
    b_high, b_low = split2(b)
    return lax.dot_general(
        jnp.concatenate([a_high, a_low, a_high], axis=0),
        jnp.concatenate([b_high, b_high, b_low], axis=0),
        (((0,), (0,)), ((), ())),
        preferred_element_type=jnp.float32,
    )


def dot(a, b):
    return jnp.dot(a, b, precision=HIGHEST, preferred_element_type=jnp.float32)


def tree_send(buf, send_sems, recv_sems, tree, direction, index, rows, col):
    row = lax.axis_index("row")
    return pltpu.make_async_remote_copy(
        src_ref=buf.at[rows],
        dst_ref=buf.at[rows],
        send_sem=send_sems.at[tree, direction],
        recv_sem=recv_sems.at[tree, index],
        device_id=(row, neighbour(col, direction)),
        device_id_type=MESH,
    )


def bit(mask, col):
    return (jnp.int32(signed(mask)) >> col) & 1


def depth_of(tree, col):
    return sum(bit(mask, col) << b for b, mask in enumerate(DEPTHS[tree]))


def tree_forward(buf, send_sems, recv_sems, step, count, piece, lag, depths, col):
    for tree in range(4):
        index = step - lag * depths[tree]
        rows = pl.ds(pl.multiple_of((index * 4 + tree) * piece, piece), piece)

        @pl.when((index >= 0) & (index < count))
        def _():
            @pl.when(col != 0)
            def _():
                pltpu.make_async_copy(buf.at[rows], buf.at[rows], recv_sems.at[tree, index]).wait()

            for direction in range(4):

                @pl.when(passes(tree, direction, col))
                def _():
                    tree_send(buf, send_sems, recv_sems, tree, direction, index, rows, col).start()


def tree_drain(buf, send_sems, recv_sems, total, col):
    for tree in range(4):
        for direction in range(4):

            @pl.when(passes(tree, direction, col))
            def _():
                tree_send(
                    buf, send_sems, recv_sems, tree, direction, 0, pl.ds(0, total), col
                ).wait_send()


def invert_pair(one, two):
    half = one.shape[0]
    width = 128
    spare = [jnp.zeros((8, width - 2 * half), jnp.float32)] if width > 2 * half else []
    xs = [
        jnp.concatenate([one[i : i + 8], two[i : i + 8]] + spare, axis=1)
        for i in range(0, half, 8)
    ]
    lane = lax.broadcasted_iota(jnp.int32, (8, width), 1)
    index = lax.broadcasted_iota(jnp.int32, (8, width), 0)
    right = lane >= half
    offset = lax.rem(lane, half)
    base = lane - offset
    right_row, offset_row = right[:1], offset[:1]

    def column(x, k):
        return jnp.take_along_axis(x, base + k, axis=1)

    for k in range(0, half, 2):
        home, s = k // 8, k % 8
        c0 = [column(x, k) for x in xs]
        c1 = [column(x, k + 1) for x in xs]
        a, b = c0[home][s : s + 1], c1[home][s : s + 1]
        c, d = c0[home][s + 1 : s + 2], c1[home][s + 1 : s + 2]
        det = a * d - b * c
        inv = 1.0 / det
        in_pair = (offset == k) | (offset == k + 1)
        first, second = offset_row == k, offset_row == k + 1
        r0, r1 = xs[home][s : s + 1], xs[home][s + 1 : s + 2]
        r0 = jnp.where(first, 1.0, jnp.where(second, 0.0, r0))
        r1 = jnp.where(first, 0.0, jnp.where(second, 1.0, r1))
        w0 = (d * r0 - b * r1) * inv
        w1 = (a * r1 - c * r0) * inv
        w0b, w1b = jnp.broadcast_to(w0, (8, width)), jnp.broadcast_to(w1, (8, width))
        u0b, u1b = jnp.where(right, w0b, 0.0), jnp.where(right, w1b, 0.0)
        clear = in_pair & right
        ra = lax.rsqrt(a)
        top = jnp.broadcast_to(jnp.where(right_row, w0, r0 * ra), (8, width))
        low = jnp.broadcast_to(
            w1 * jnp.where(right_row, 1.0, ra * jnp.sqrt(jnp.where(right_row, 1.0, det))),
            (8, width),
        )
        for i, x in enumerate(xs):
            if i < home:
                new = jnp.where(clear, 0.0, x) - (c0[i] * u0b + c1[i] * u1b)
            elif i > home:
                new = jnp.where(in_pair, 0.0, x) - (c0[i] * w0b + c1[i] * w1b)
            else:
                moves = right | (index > s)
                new = jnp.where(in_pair & moves, 0.0, x) - jnp.where(
                    moves, c0[i] * w0b + c1[i] * w1b, 0.0
                )
                new = jnp.where(index == s, top, new)
                new = jnp.where(index == s + 1, low, new)
            xs[i] = new
    return jnp.concatenate(xs, axis=0)


def factor(g, top, out, chol, gj):
    b = BLOCK
    blocks = PANEL // b
    eye = jnp.eye(b, dtype=jnp.float32)
    lower = lax.broadcasted_iota(jnp.int32, (b, b), 0) >= lax.broadcasted_iota(
        jnp.int32, (b, b), 1
    )
    chol[...] = jnp.zeros_like(chol)
    gj[...] = jnp.zeros_like(gj)

    for step in range(blocks + 1):
        one, two = eye, eye
        if step < blocks:
            lo, hi = step * b, (step + 1) * b
            left = g[lo:hi, lo:PANEL]
            wide = [left]
            if step > 0:
                prod = dot_t(chol[:lo, lo:hi], chol[:lo, lo : PANEL + lo])
                left = left - prod[:, : PANEL - lo]
                wide = [left, -prod[:, PANEL - lo :]]
            wide.append(eye)
            one = left[:, :b]
        if step > 0:
            glo, ghi = (step - 1) * b, step * b
            work = chol[glo:ghi, :PANEL] + top[glo:ghi, :PANEL]
            gwide = [work]
            if glo > 0:
                prod = dot(work[:, :glo], gj[:glo, glo : PANEL + glo])
                work = work[:, glo:] - prod[:, : PANEL - glo]
                gwide = [work, -prod[:, PANEL - glo :]]
            gwide.append(eye)
            two = work[:, :b]
        both = invert_pair(one, two)
        if step < blocks:
            inv = jnp.where(lower, both[:, :b], 0.0)
            chol[lo:hi, lo : PANEL + hi] = dot(inv, jnp.concatenate(wide, axis=1))
        if step > 0:
            new = dot(both[:, b : 2 * b], jnp.concatenate(gwide, axis=1))
            if glo > 0:
                gj[:glo, glo : PANEL + ghi] -= dot(gj[:glo, glo:ghi], new)
            gj[glo:ghi, glo : PANEL + ghi] = new
    out[:PANEL] = chol[:, PANEL:]
    out[PANEL:] = gj[:, PANEL:]


def gather_kernel(
    a_hbm,
    p_hbm,
    z_out,
    x_out,
    a,
    p,
    part,
    slots,
    total,
    top,
    tree_sends,
    tree_recvs,
    rs_sends,
    rs_recvs,
    ag_sends,
    ag_recvs,
    share_sends,
    share_recv,
    top_sends,
    top_recvs,
    local_sems,
    f,
    chol,
    gj,
    f_sends,
    f_recvs,
    half,
):
    row, col = lax.axis_index("row"), lax.axis_index("col")
    rows, width = a.shape
    share = PANEL // ROW
    macro = PANEL
    count = rows // macro
    per_macro = macro // (4 * PIECE)

    panel_copy = pltpu.make_async_copy(a_hbm.at[:, pl.ds(0, PANEL)], p, local_sems.at[0])
    loads = [
        pltpu.make_async_copy(
            a_hbm.at[pl.ds(i * PANEL, PANEL)], a.at[pl.ds(i * PANEL, PANEL)], local_sems.at[1 + i]
        )
        for i in range(count)
    ]

    @pl.when(col == 0)
    def _():
        panel_copy.start()

    for load in loads:
        load.start()

    barrier = pltpu.get_barrier_semaphore()
    peers = [lax.rem(row + d, ROW) for d in range(1, ROW)]
    for peer in peers:
        pl.semaphore_signal(barrier, inc=1, device_id=(peer, col), device_id_type=MESH)
    for direction in range(4):
        pl.semaphore_signal(
            barrier, inc=1, device_id=(row, neighbour(col, direction)), device_id_type=MESH
        )
    pl.semaphore_wait(barrier, len(peers) + 4)

    mine = pl.ds(pl.multiple_of(row * share, share), share)

    def share_copy(d):
        theirs = pl.ds(pl.multiple_of(peers[d] * share, share), share)
        return pltpu.make_async_remote_copy(
            src_ref=a.at[theirs],
            dst_ref=top.at[theirs],
            send_sem=share_sends.at[d],
            recv_sem=share_recv,
            device_id=(peers[d], col),
            device_id_type=MESH,
        )

    own_share = pltpu.make_async_copy(a.at[mine], top.at[mine], share_recv)

    def top_copy(d):
        return pltpu.make_async_remote_copy(
            src_ref=top.at[mine],
            dst_ref=top.at[mine],
            send_sem=top_sends.at[d],
            recv_sem=top_recvs.at[d],
            device_id=(peers[d], col),
            device_id_type=MESH,
        )

    loads[0].wait()

    @pl.when(row == 0)
    def _():
        own_share.start()
        for d in range(ROW - 1):
            share_copy(d).start()

    @pl.when(col == 0)
    def _():
        panel_copy.wait()

    for load in loads[1:]:
        load.wait()

    part[...] = jnp.zeros_like(part)
    half[...] = jnp.zeros_like(half)

    depths = [depth_of(tree, col) for tree in range(4)]
    deepest = functools.reduce(jnp.maximum, depths)
    pieces = count * per_macro

    @pl.loop(0, pieces + LAG * deepest)
    def _(step):
        tree_forward(p, tree_sends, tree_recvs, step, pieces, PIECE, LAG, depths, col)
        due = step - LAG * deepest + 1

        @pl.when(step == TOP_STEP)
        def _():
            own_share.wait()
            for d in range(ROW - 1):
                top_copy(d).start()

        @pl.when((due > 0) & (lax.rem(due, per_macro) == 0))
        def _():
            i = lax.div(due, per_macro) - 1
            block = pl.ds(pl.multiple_of(i * macro, macro), macro)

            @pl.when(col == 0)
            def _():
                high, low = split2(p[block])
                rest = p[block] - high.astype(jnp.float32) - low.astype(jnp.float32)
                part[:, :PANEL] += dot_t(
                    jnp.concatenate([high, low], axis=0), jnp.concatenate([high, low], axis=0)
                )
                half[...] += dot_t(
                    jnp.concatenate([high, high], axis=0),
                    jnp.concatenate([low, rest.astype(jnp.bfloat16)], axis=0),
                )
                part[:, PANEL:] += dot_t_split(p[block], a[block, PANEL:])

            @pl.when(col != 0)
            def _():
                part[...] += dot_t_split(p[block], a[block])

            pltpu.make_async_copy(p.at[block], p_hbm.at[block], local_sems.at[0]).start()

    @pl.when(col == 0)
    def _():
        part[:, :PANEL] += half[...] + half[...].T

    def part_copy(d):
        return pltpu.make_async_remote_copy(
            src_ref=part.at[pl.ds(pl.multiple_of(peers[d] * share, share), share)],
            dst_ref=slots.at[d],
            send_sem=rs_sends.at[d],
            recv_sem=rs_recvs.at[d],
            device_id=(peers[d], col),
            device_id_type=MESH,
        )

    def sum_copy(d):
        return pltpu.make_async_remote_copy(
            src_ref=total.at[mine],
            dst_ref=total.at[mine],
            send_sem=ag_sends.at[d],
            recv_sem=ag_recvs.at[d],
            device_id=(peers[d], col),
            device_id_type=MESH,
        )

    for d in range(ROW - 1):
        part_copy(d).start()

    acc = part[mine]
    for d in range(ROW - 1):
        part_copy(d).wait_recv()
        acc += slots[d]
    total[mine] = acc
    for d in range(ROW - 1):
        sum_copy(d).start()


    def sums_and_top():
        for d in range(ROW - 1):
            sum_copy(d).wait_recv()
            top_copy(d).wait_recv()

    @pl.when(col == 0)
    def _():
        sums_and_top()
        factor(total, top, f, chol, gj)

    small = 2 * PANEL // (4 * SMALL)

    @pl.loop(0, small + SMALL_LAG * deepest)
    def _(step):
        tree_forward(f, f_sends, f_recvs, step, small, SMALL, SMALL_LAG, depths, col)

    @pl.when(col != 0)
    def _():
        sums_and_top()

    z = dot_split(f[:PANEL], total[...])
    z_out[...] = z
    x_out[...] = dot_split(f[PANEL:], z + top[...])

    for d in range(ROW - 1):
        top_copy(d).wait_send()

    @pl.when(row == 0)
    def _():
        for d in range(ROW - 1):
            share_copy(d).wait_send()

    for d in range(ROW - 1):
        part_copy(d).wait_send()
        sum_copy(d).wait_send()
    tree_drain(p, tree_sends, tree_recvs, rows // 4, col)
    tree_drain(f, f_sends, f_recvs, 2 * PANEL // 4, col)
    pltpu.make_async_copy(p, p_hbm, local_sems.at[0]).wait()


def gather(matrix):
    rows, width = matrix.shape
    count = rows // PANEL
    dma = pltpu.SemaphoreType.DMA
    return pl.pallas_call(
        gather_kernel,
        name="gather",
        out_shape=(
            jax.ShapeDtypeStruct((rows, PANEL), jnp.float32),
            jax.ShapeDtypeStruct((PANEL, width), jnp.float32),
            jax.ShapeDtypeStruct((PANEL, width), jnp.float32),
        ),
        in_specs=[pl.BlockSpec(memory_space=pl.ANY)],
        out_specs=(
            pl.BlockSpec(memory_space=pl.ANY),
            pl.BlockSpec(memory_space=pltpu.VMEM),
            pl.BlockSpec(memory_space=pltpu.VMEM),
        ),
        scratch_shapes=[
            pltpu.VMEM((rows, width), jnp.float32),
            pltpu.VMEM((rows, PANEL), jnp.float32),
            pltpu.VMEM((PANEL, width), jnp.float32),
            pltpu.VMEM((ROW - 1, PANEL // ROW, width), jnp.float32),
            pltpu.VMEM((PANEL, width), jnp.float32),
            pltpu.VMEM((PANEL, width), jnp.float32),
            dma((4, 4)),
            dma((4, rows // (4 * PIECE))),
            dma((ROW - 1,)),
            dma((ROW - 1,)),
            dma((ROW - 1,)),
            dma((ROW - 1,)),
            dma((ROW - 1,)),
            dma(()),
            dma((ROW - 1,)),
            dma((ROW - 1,)),
            dma((1 + count,)),
            pltpu.VMEM((2 * PANEL, PANEL), jnp.float32),
            pltpu.VMEM((PANEL, 2 * PANEL), jnp.float32),
            pltpu.VMEM((PANEL, 2 * PANEL), jnp.float32),
            dma((4, 4)),
            dma((4, 2 * PANEL // (4 * SMALL))),
            pltpu.VMEM((PANEL, PANEL), jnp.float32),
        ],
        compiler_params=pltpu.CompilerParams(
            collective_id=0, has_side_effects=True, vmem_limit_bytes=48 << 20
        ),
    )(matrix)


TILE = 512


def update_kernel(a, p, z, x, out):
    out[...] = a[...] - dot_split(p[...], x[...])

    @pl.when((lax.axis_index("row") == 0) & (pl.program_id(0) == 0))
    def _():
        out[:PANEL] = -z[...]


def update(matrix, panel, z, x):
    rows, width = matrix.shape
    whole = pl.BlockSpec((PANEL, width), lambda i: (0, 0))
    return pl.pallas_call(
        update_kernel,
        name="update",
        out_shape=jax.ShapeDtypeStruct(matrix.shape, jnp.float32),
        grid=(rows // TILE,),
        in_specs=[
            pl.BlockSpec((TILE, width), lambda i: (i, 0)),
            pl.BlockSpec((TILE, PANEL), lambda i: (i, 0)),
            whole,
            whole,
        ],
        out_specs=pl.BlockSpec((TILE, width), lambda i: (i, 0)),
    )(matrix, panel, z, x)


def on_device(matrix):
    panel, z, x = gather(matrix)
    return update(matrix, panel, z, x)


def solution(mesh):
    in_specs = (P("row", "col"),)
    out_specs = P("row", "col")
    return jax.shard_map(
        on_device, mesh=mesh, in_specs=in_specs, out_specs=out_specs, check_vma=False
    )
```

```python
import functools

import jax
import jax.numpy as jnp
from jax import lax
from jax.experimental import pallas as pl
from jax.experimental.pallas import tpu as pltpu
from jax.sharding import PartitionSpec as P

PANEL = 256
Y, Z = 4, 8
ROW = 8
PIECE = 32
BLOCK = 32
SMALL = 32
SMALL_LAG = 4
MESH = pl.DeviceIdType.MESH
HIGHEST = lax.Precision.HIGHEST

TREES = (
    (205809287, 1078206464, 153162274, 1145052164),
    (2425421888, 2348828425, 538199108, 2291729160),
    (1646792752, 573083664, 1082827025, 536928418),
    (16943360, 294848740, 2252343432, 321257537),
)
DEPTHS = (
    (1515870810, 3552543676, 3221224912),
    (1515870810, 3647453556, 671088562),
    (1515870810, 2381649390, 4294962692),
    (1515870810, 3474847550, 1693450230),
)
TOP_STEP = 8
LAG = 4


def signed(mask):
    return mask - (1 << 32) if mask >= 1 << 31 else mask


def passes(tree, direction, col):
    return (jnp.int32(signed(TREES[tree][direction])) >> col) & 1 == 1


def neighbour(col, direction):
    y, z = lax.rem(col, Y), lax.div(col, Y)
    if direction == 0:
        y = lax.rem(y + 1, Y)
    elif direction == 1:
        y = lax.rem(y + Y - 1, Y)
    elif direction == 2:
        z = lax.rem(z + 1, Z)
    else:
        z = lax.rem(z + Z - 1, Z)
    return z * Y + y


def dot_t(a, b):
    precision = HIGHEST if a.dtype == jnp.float32 else None
    return lax.dot_general(
        a, b, (((0,), (0,)), ((), ())), precision=precision, preferred_element_type=jnp.float32
    )


def split2(x):
    high = x.astype(jnp.bfloat16)
    return high, (x - high.astype(jnp.float32)).astype(jnp.bfloat16)


def dot_split(a, b):
    a_high, a_low = split2(a)
    b_high, b_low = split2(b)
    return jnp.dot(
        jnp.concatenate([a_high, a_low, a_high], axis=1),
        jnp.concatenate([b_high, b_high, b_low], axis=0),
        preferred_element_type=jnp.float32,
    )


def dot_t_split(a, b):
    a_high, a_low = split2(a)
    b_high, b_low = split2(b)
    return lax.dot_general(
        jnp.concatenate([a_high, a_low, a_high], axis=0),
        jnp.concatenate([b_high, b_high, b_low], axis=0),
        (((0,), (0,)), ((), ())),
        preferred_element_type=jnp.float32,
    )


def dot(a, b):
    return jnp.dot(a, b, precision=HIGHEST, preferred_element_type=jnp.float32)


def tree_send(buf, send_sems, recv_sems, tree, direction, index, rows, col):
    row = lax.axis_index("row")
    return pltpu.make_async_remote_copy(
        src_ref=buf.at[rows],
        dst_ref=buf.at[rows],
        send_sem=send_sems.at[tree, direction],
        recv_sem=recv_sems.at[tree, index],
        device_id=(row, neighbour(col, direction)),
        device_id_type=MESH,
    )


def bit(mask, col):
    return (jnp.int32(signed(mask)) >> col) & 1


def depth_of(tree, col):
    return sum(bit(mask, col) << b for b, mask in enumerate(DEPTHS[tree]))


def tree_forward(buf, send_sems, recv_sems, step, count, piece, lag, depths, col):
    for tree in range(4):
        index = step - lag * depths[tree]
        rows = pl.ds(pl.multiple_of((index * 4 + tree) * piece, piece), piece)

        @pl.when((index >= 0) & (index < count))
        def _():
            @pl.when(col != 0)
            def _():
                pltpu.make_async_copy(buf.at[rows], buf.at[rows], recv_sems.at[tree, index]).wait()

            for direction in range(4):

                @pl.when(passes(tree, direction, col))
                def _():
                    tree_send(buf, send_sems, recv_sems, tree, direction, index, rows, col).start()


def tree_drain(buf, send_sems, recv_sems, total, col):
    for tree in range(4):
        for direction in range(4):

            @pl.when(passes(tree, direction, col))
            def _():
                tree_send(
                    buf, send_sems, recv_sems, tree, direction, 0, pl.ds(0, total), col
                ).wait_send()


def invert_pair(one, two):
    half = one.shape[0]
    width = 128
    spare = [jnp.zeros((8, width - 2 * half), jnp.float32)] if width > 2 * half else []
    xs = [
        jnp.concatenate([one[i : i + 8], two[i : i + 8]] + spare, axis=1)
        for i in range(0, half, 8)
    ]
    lane = lax.broadcasted_iota(jnp.int32, (8, width), 1)
    index = lax.broadcasted_iota(jnp.int32, (8, width), 0)
    right = lane >= half
    offset = lax.rem(lane, half)
    base = lane - offset
    right_row, offset_row = right[:1], offset[:1]

    def column(x, k):
        return jnp.take_along_axis(x, base + k, axis=1)

    for k in range(0, half, 2):
        home, s = k // 8, k % 8
        c0 = [column(x, k) for x in xs]
        c1 = [column(x, k + 1) for x in xs]
        a, b = c0[home][s : s + 1], c1[home][s : s + 1]
        c, d = c0[home][s + 1 : s + 2], c1[home][s + 1 : s + 2]
        det = a * d - b * c
        inv = 1.0 / det
        in_pair = (offset == k) | (offset == k + 1)
        first, second = offset_row == k, offset_row == k + 1
        r0, r1 = xs[home][s : s + 1], xs[home][s + 1 : s + 2]
        r0 = jnp.where(first, 1.0, jnp.where(second, 0.0, r0))
        r1 = jnp.where(first, 0.0, jnp.where(second, 1.0, r1))
        w0 = (d * r0 - b * r1) * inv
        w1 = (a * r1 - c * r0) * inv
        w0b, w1b = jnp.broadcast_to(w0, (8, width)), jnp.broadcast_to(w1, (8, width))
        u0b, u1b = jnp.where(right, w0b, 0.0), jnp.where(right, w1b, 0.0)
        clear = in_pair & right
        ra = lax.rsqrt(a)
        top = jnp.broadcast_to(jnp.where(right_row, w0, r0 * ra), (8, width))
        low = jnp.broadcast_to(
            w1 * jnp.where(right_row, 1.0, ra * jnp.sqrt(jnp.where(right_row, 1.0, det))),
            (8, width),
        )
        for i, x in enumerate(xs):
            if i < home:
                new = jnp.where(clear, 0.0, x) - (c0[i] * u0b + c1[i] * u1b)
            elif i > home:
                new = jnp.where(in_pair, 0.0, x) - (c0[i] * w0b + c1[i] * w1b)
            else:
                moves = right | (index > s)
                new = jnp.where(in_pair & moves, 0.0, x) - jnp.where(
                    moves, c0[i] * w0b + c1[i] * w1b, 0.0
                )
                new = jnp.where(index == s, top, new)
                new = jnp.where(index == s + 1, low, new)
            xs[i] = new
    return jnp.concatenate(xs, axis=0)


def factor(g, top, out, chol, gj):
    b = BLOCK
    blocks = PANEL // b
    eye = jnp.eye(b, dtype=jnp.float32)
    lower = lax.broadcasted_iota(jnp.int32, (b, b), 0) >= lax.broadcasted_iota(
        jnp.int32, (b, b), 1
    )
    chol[...] = jnp.zeros_like(chol)
    gj[...] = jnp.zeros_like(gj)

    for step in range(blocks + 1):
        one, two = eye, eye
        if step < blocks:
            lo, hi = step * b, (step + 1) * b
            left = g[lo:hi, lo:PANEL]
            wide = [left]
            if step > 0:
                prod = dot_t(chol[:lo, lo:hi], chol[:lo, lo : PANEL + lo])
                left = left - prod[:, : PANEL - lo]
                wide = [left, -prod[:, PANEL - lo :]]
            wide.append(eye)
            one = left[:, :b]
        if step > 0:
            glo, ghi = (step - 1) * b, step * b
            work = chol[glo:ghi, :PANEL] + top[glo:ghi, :PANEL]
            gwide = [work]
            if glo > 0:
                prod = dot(work[:, :glo], gj[:glo, glo : PANEL + glo])
                work = work[:, glo:] - prod[:, : PANEL - glo]
                gwide = [work, -prod[:, PANEL - glo :]]
            gwide.append(eye)
            two = work[:, :b]
        both = invert_pair(one, two)
        if step < blocks:
            inv = jnp.where(lower, both[:, :b], 0.0)
            chol[lo:hi, lo : PANEL + hi] = dot(inv, jnp.concatenate(wide, axis=1))
        if step > 0:
            new = dot(both[:, b : 2 * b], jnp.concatenate(gwide, axis=1))
            if glo > 0:
                gj[:glo, glo : PANEL + ghi] -= dot(gj[:glo, glo:ghi], new)
            gj[glo:ghi, glo : PANEL + ghi] = new
    out[:PANEL] = chol[:, PANEL:]
    out[PANEL:] = gj[:, PANEL:]


def gather_kernel(
    a_hbm,
    p_hbm,
    z_out,
    x_out,
    a,
    p,
    part,
    slots,
    total,
    top,
    tree_sends,
    tree_recvs,
    rs_sends,
    rs_recvs,
    ag_sends,
    ag_recvs,
    share_sends,
    share_recv,
    top_sends,
    top_recvs,
    local_sems,
    f,
    chol,
    gj,
    f_sends,
    f_recvs,
    half,
):
    row, col = lax.axis_index("row"), lax.axis_index("col")
    rows, width = a.shape
    share = PANEL // ROW
    macro = PANEL
    count = rows // macro
    per_macro = macro // (4 * PIECE)

    panel_copy = pltpu.make_async_copy(a_hbm.at[:, pl.ds(0, PANEL)], p, local_sems.at[0])
    loads = [
        pltpu.make_async_copy(
            a_hbm.at[pl.ds(i * PANEL, PANEL)], a.at[pl.ds(i * PANEL, PANEL)], local_sems.at[1 + i]
        )
        for i in range(count)
    ]

    @pl.when(col == 0)
    def _():
        panel_copy.start()

    for load in loads:
        load.start()

    barrier = pltpu.get_barrier_semaphore()
    peers = [lax.rem(row + d, ROW) for d in range(1, ROW)]
    for peer in peers:
        pl.semaphore_signal(barrier, inc=1, device_id=(peer, col), device_id_type=MESH)
    for direction in range(4):
        pl.semaphore_signal(
            barrier, inc=1, device_id=(row, neighbour(col, direction)), device_id_type=MESH
        )
    pl.semaphore_wait(barrier, len(peers) + 4)

    mine = pl.ds(pl.multiple_of(row * share, share), share)

    def share_copy(d):
        theirs = pl.ds(pl.multiple_of(peers[d] * share, share), share)
        return pltpu.make_async_remote_copy(
            src_ref=a.at[theirs],
            dst_ref=top.at[theirs],
            send_sem=share_sends.at[d],
            recv_sem=share_recv,
            device_id=(peers[d], col),
            device_id_type=MESH,
        )

    own_share = pltpu.make_async_copy(a.at[mine], top.at[mine], share_recv)

    def top_copy(d):
        return pltpu.make_async_remote_copy(
            src_ref=top.at[mine],
            dst_ref=top.at[mine],
            send_sem=top_sends.at[d],
            recv_sem=top_recvs.at[d],
            device_id=(peers[d], col),
            device_id_type=MESH,
        )

    loads[0].wait()

    @pl.when(row == 0)
    def _():
        own_share.start()
        for d in range(ROW - 1):
            share_copy(d).start()

    @pl.when(col == 0)
    def _():
        panel_copy.wait()

    for load in loads[1:]:
        load.wait()

    part[...] = jnp.zeros_like(part)
    half[...] = jnp.zeros_like(half)

    depths = [depth_of(tree, col) for tree in range(4)]
    deepest = functools.reduce(jnp.maximum, depths)
    pieces = count * per_macro

    @pl.loop(0, pieces + LAG * deepest)
    def _(step):
        tree_forward(p, tree_sends, tree_recvs, step, pieces, PIECE, LAG, depths, col)
        due = step - LAG * deepest + 1

        @pl.when(step == TOP_STEP)
        def _():
            own_share.wait()
            for d in range(ROW - 1):
                top_copy(d).start()

        @pl.when((due > 0) & (lax.rem(due, per_macro) == 0))
        def _():
            i = lax.div(due, per_macro) - 1
            block = pl.ds(pl.multiple_of(i * macro, macro), macro)

            @pl.when(col == 0)
            def _():
                high, low = split2(p[block])
                rest = p[block] - high.astype(jnp.float32) - low.astype(jnp.float32)
                part[:, :PANEL] += dot_t(
                    jnp.concatenate([high, low], axis=0), jnp.concatenate([high, low], axis=0)
                )
                half[...] += dot_t(
                    jnp.concatenate([high, high], axis=0),
                    jnp.concatenate([low, rest.astype(jnp.bfloat16)], axis=0),
                )
                part[:, PANEL:] += dot_t_split(p[block], a[block, PANEL:])

            @pl.when(col != 0)
            def _():
                part[...] += dot_t_split(p[block], a[block])

            pltpu.make_async_copy(p.at[block], p_hbm.at[block], local_sems.at[0]).start()

    @pl.when(col == 0)
    def _():
        part[:, :PANEL] += half[...] + half[...].T

    def part_copy(d):
        return pltpu.make_async_remote_copy(
            src_ref=part.at[pl.ds(pl.multiple_of(peers[d] * share, share), share)],
            dst_ref=slots.at[d],
            send_sem=rs_sends.at[d],
            recv_sem=rs_recvs.at[d],
            device_id=(peers[d], col),
            device_id_type=MESH,
        )

    def sum_copy(d):
        return pltpu.make_async_remote_copy(
            src_ref=total.at[mine],
            dst_ref=total.at[mine],
            send_sem=ag_sends.at[d],
            recv_sem=ag_recvs.at[d],
            device_id=(peers[d], col),
            device_id_type=MESH,
        )

    for d in range(ROW - 1):
        part_copy(d).start()

    acc = part[mine]
    for d in range(ROW - 1):
        part_copy(d).wait_recv()
        acc += slots[d]
    total[mine] = acc
    for d in range(ROW - 1):
        sum_copy(d).start()


    def sums_and_top():
        for d in range(ROW - 1):
            sum_copy(d).wait_recv()
            top_copy(d).wait_recv()

    @pl.when(col == 0)
    def _():
        sums_and_top()
        factor(total, top, f, chol, gj)

    small = 2 * PANEL // (4 * SMALL)

    @pl.loop(0, small + SMALL_LAG * deepest)
    def _(step):
        tree_forward(f, f_sends, f_recvs, step, small, SMALL, SMALL_LAG, depths, col)

    @pl.when(col != 0)
    def _():
        sums_and_top()

    z = dot_split(f[:PANEL], total[...])
    z_out[...] = z
    x_out[...] = dot_split(f[PANEL:], z + top[...])

    for d in range(ROW - 1):
        top_copy(d).wait_send()

    @pl.when(row == 0)
    def _():
        for d in range(ROW - 1):
            share_copy(d).wait_send()

    for d in range(ROW - 1):
        part_copy(d).wait_send()
        sum_copy(d).wait_send()
    tree_drain(p, tree_sends, tree_recvs, rows // 4, col)
    tree_drain(f, f_sends, f_recvs, 2 * PANEL // 4, col)
    pltpu.make_async_copy(p, p_hbm, local_sems.at[0]).wait()


def gather(matrix):
    rows, width = matrix.shape
    count = rows // PANEL
    dma = pltpu.SemaphoreType.DMA
    return pl.pallas_call(
        gather_kernel,
        name="gather",
        out_shape=(
            jax.ShapeDtypeStruct((rows, PANEL), jnp.float32),
            jax.ShapeDtypeStruct((PANEL, width), jnp.float32),
            jax.ShapeDtypeStruct((PANEL, width), jnp.float32),
        ),
        in_specs=[pl.BlockSpec(memory_space=pl.ANY)],
        out_specs=(
            pl.BlockSpec(memory_space=pl.ANY),
            pl.BlockSpec(memory_space=pltpu.VMEM),
            pl.BlockSpec(memory_space=pltpu.VMEM),
        ),
        scratch_shapes=[
            pltpu.VMEM((rows, width), jnp.float32),
            pltpu.VMEM((rows, PANEL), jnp.float32),
            pltpu.VMEM((PANEL, width), jnp.float32),
            pltpu.VMEM((ROW - 1, PANEL // ROW, width), jnp.float32),
            pltpu.VMEM((PANEL, width), jnp.float32),
            pltpu.VMEM((PANEL, width), jnp.float32),
            dma((4, 4)),
            dma((4, rows // (4 * PIECE))),
            dma((ROW - 1,)),
            dma((ROW - 1,)),
            dma((ROW - 1,)),
            dma((ROW - 1,)),
            dma((ROW - 1,)),
            dma(()),
            dma((ROW - 1,)),
            dma((ROW - 1,)),
            dma((1 + count,)),
            pltpu.VMEM((2 * PANEL, PANEL), jnp.float32),
            pltpu.VMEM((PANEL, 2 * PANEL), jnp.float32),
            pltpu.VMEM((PANEL, 2 * PANEL), jnp.float32),
            dma((4, 4)),
            dma((4, 2 * PANEL // (4 * SMALL))),
            pltpu.VMEM((PANEL, PANEL), jnp.float32),
        ],
        compiler_params=pltpu.CompilerParams(
            collective_id=0, has_side_effects=True, vmem_limit_bytes=48 << 20
        ),
    )(matrix)


TILE = 1024


def update_kernel(a, p, z, x, out):
    out[...] = a[...] - dot_split(p[...], x[...])

    @pl.when((lax.axis_index("row") == 0) & (pl.program_id(0) == 0))
    def _():
        out[:PANEL] = -z[...]


def update(matrix, panel, z, x):
    rows, width = matrix.shape
    whole = pl.BlockSpec((PANEL, width), lambda i: (0, 0))
    return pl.pallas_call(
        update_kernel,
        name="update",
        out_shape=jax.ShapeDtypeStruct(matrix.shape, jnp.float32),
        grid=(rows // TILE,),
        in_specs=[
            pl.BlockSpec((TILE, width), lambda i: (i, 0)),
            pl.BlockSpec((TILE, PANEL), lambda i: (i, 0)),
            whole,
            whole,
        ],
        out_specs=pl.BlockSpec((TILE, width), lambda i: (i, 0)),
    )(matrix, panel, z, x)


def on_device(matrix):
    panel, z, x = gather(matrix)
    return update(matrix, panel, z, x)


def solution(mesh):
    in_specs = (P("row", "col"),)
    out_specs = P("row", "col")
    return jax.shard_map(
        on_device, mesh=mesh, in_specs=in_specs, out_specs=out_specs, check_vma=False
    )
```
